32 devices in a mesh: ex: 4 (over y, x), ey: 2 (over core), tp: 4 (over z).
Axes of the slice: x: 2, y: 2, z: 4, core: 2. Of those that a mesh axis runs over, the one named last changes fastest.
Arguments:
- tokens: bfloat16 [256, 7168], P(('ex', 'ey'), 'tp'), may hold values from -6 to 6
- cotangent: bfloat16 [256, 7168], P(('ex', 'ey'), 'tp'), may hold values from -0.59765625 to 0.59765625
- gates: bfloat16 [256, 8], P(('ex', 'ey')), may hold values from 0.049804688 to 1
- expert_ids: int32 [256, 8], P(('ex', 'ey')), may hold values from 0 to 31, all different within a row; in each aligned block of 32 rows (0 to 31, 32 to 63, ...) at most 10 rows name the same one
- saved_gate: bfloat16 [1024, 32, 80], P(None, ('ex', 'ey')), may hold values from -6 to 6
- saved_up: bfloat16 [1024, 32, 80], P(None, ('ex', 'ey')), may hold values from -6 to 6
- w_gate: bfloat16 [32, 7168, 1024], P(('ex', 'ey'), 'tp'), may hold values from -0.1875 to 0.1875
- w_up: bfloat16 [32, 7168, 1024], P(('ex', 'ey'), 'tp'), may hold values from -0.1875 to 0.1875
- w_down: bfloat16 [32, 1024, 7168], P(('ex', 'ey'), None, 'tp'), may hold values from -0.25 to 0.25
Outputs:
- grad_tokens: bfloat16 [256, 7168], P(('ex', 'ey'), 'tp')
- grad_gates: bfloat16 [256, 8], P(('ex', 'ey'))
- grad_w_gate: bfloat16 [32, 7168, 1024], P(('ex', 'ey'), 'tp')
- grad_w_up: bfloat16 [32, 7168, 1024], P(('ex', 'ey'), 'tp')
- grad_w_down: bfloat16 [32, 1024, 7168], P(('ex', 'ey'), None, 'tp')
The draws below stay inside these ranges and needn't reach their ends.
Inputs may be any that keep to these rules, and one draw needn't show every extreme that they name: `expert_ids`: each row names 8 different experts. The rows of one token group name any one expert at most 10 times, a bound that some block reaches.
All inputs are finite; a program needn't handle non-finite values.
Results may differ from the reference program's by a relative error of at most 0.025.
Values may be sent and summed in bfloat16 or wider, within the bound.
A program may use at most 128 MiB of HBM per device.

```python
import math
import jax
import jax.numpy as jnp
import numpy as np
from jax import lax

D = 7168
FF = 1024
EXPERTS = 32
TOP = 8
TOK_DEV = 32
CAP = 10
SLOTS = 80
TOKENS = 256
N_EX = 4
N_EY = 2
N_TP = 4


def spiked(entries, rng, source, target, blocks, factor):
    owner, partner = [(jnp.arange(entries.shape[dim]) // (entries.shape[dim] // blocks)).reshape([-1 if axis == dim else 1 for axis in range(entries.ndim)]) for dim in (source, target)]
    chosen = jax.random.permutation(rng, blocks)[partner]
    strong = (owner == chosen) | (owner == (partner + blocks // 2) % blocks)
    return jnp.where(strong, factor * entries, entries)


def levels(stream_key, shape, shards, low, high):
    gain, own = 1.0, jax.random.fold_in(stream_key, 6)
    for dim, parts in shards:
        draws = jnp.exp(jax.random.uniform(jax.random.fold_in(own, dim), (parts,), jnp.float32, low / len(shards), high / len(shards)))
        gain = gain * jnp.repeat(draws, shape[dim] // parts).reshape([-1 if axis == dim else 1 for axis in range(len(shape))])
    return gain


def assign_block(own_key, own, number, rows, count, top, most, skew):
    ranking = jax.random.permutation(own_key, count)
    heavy_load, usual = shares(count, rows * top, most, skew, True), shares(count, rows * top, most, skew, False)
    places = jnp.arange(count)

    def named(lengths, rotation):
        used = int((lengths > 0).sum())
        fixed = max(1, used // 4)
        moved = fixed + (places - fixed + rotation * (used - fixed)) % max(1, count - fixed)
        return jnp.zeros((count,), jnp.int32).at[ranking[jnp.where(places < fixed, places, moved)]].set(jnp.asarray(lengths, jnp.int32))

    lengths = jnp.where(number % 4 == 0, named(heavy_load, number // 4), named(usual, number - number // 4 - 1))
    mixed = jax.random.permutation(jax.random.fold_in(own, 3), count)
    donor, receiver = mixed[0:count // 2 * 2:2], mixed[1:count // 2 * 2:2]
    room = jnp.minimum(lengths[donor] - 1, most - lengths[receiver]) // 2
    room = jnp.where((donor == ranking[0]) | (receiver == ranking[0]) | (lengths[receiver] == 0), 0, jnp.maximum(room, 0))
    moved = jax.random.randint(jax.random.fold_in(own, 4), (count // 2,), 0, 1 << 20) % (room + 1)
    lengths = lengths.at[donor].add(-moved).at[receiver].add(moved)
    labels = jnp.searchsorted(jnp.cumsum(lengths), jnp.arange(rows * top), side="right").astype(jnp.int32)
    table = labels.reshape(top, rows).T
    table = table[jax.random.permutation(jax.random.fold_in(own, 1), rows)]
    rotation = jax.random.randint(jax.random.fold_in(own, 2), (rows, 1), 0, top)
    return jnp.take_along_axis(table, (jnp.arange(top)[None, :] + rotation) % top, axis=1)


def shares(count, total, most, skew, full):
    weights = [(1 << 20) // math.isqrt(standing ** skew) + 1 for standing in range(1, count + 1)]
    largest = most if full else min(most, max(-(-total // count), total * weights[0] // sum(weights)))
    least = 1 if total - largest >= count - 1 else 0
    holding, spare = [largest] + [least] * (count - 1), total - largest - least * (count - 1)
    while spare > 0:
        candidates = [i for i in range(1, count) if holding[i] < largest] or [i for i in range(1, count) if holding[i] < most]
        mass, budget = sum([weights[i] for i in candidates]), spare
        for i in candidates:
            addition = min(most - holding[i], max(1, budget * weights[i] // mass), spare)
            holding[i] = holding[i] + addition
            spare = spare - addition
    return np.array(holding)


def centred(stream_key, shape, deviation, limit, shards=(), kind=jnp.bfloat16):
    entries = jax.random.normal(stream_key, shape, jnp.float32) * deviation
    if len(shards) > 0:
        entries = levels(stream_key, shape, shards, -0.22, 0.18) * entries
    return jnp.clip(entries, min=-limit, max=limit).astype(kind)


def heavy_noise(key, shape, scale, limit, cuts, heavy, held_as=jnp.bfloat16):
    result = scale * jax.random.normal(key, shape, jnp.float32)
    if cuts:
        result = result * levels(key, shape, cuts, -0.22, 0.18)
    return jnp.clip(spiked(result, jax.random.fold_in(key, 3), *heavy), -limit, limit).astype(held_as)


def setup_inputs(seed: int = 0) -> dict:
    splits = jax.random.split(jax.random.key(seed), 10)
    tokens = centred(splits[0], (TOKENS, D), 1.0, 6.0, ((0, 8), (1, 4)))
    cotangent = centred(splits[1], (TOKENS, D), 0.1, 0.59765625, ((0, 8), (1, 4)))
    gates = jnp.clip(jnp.exp(math.log(1.0) - 2.9996462 * jax.random.uniform(splits[2], (TOKENS, TOP), jnp.float32) ** levels(splits[2], (TOKENS, TOP), ((0, 8),), -0.2, 0.2)), 0.049804688, 1.0).astype(jnp.bfloat16)
    expert_ids_keys = jax.random.split(jax.random.fold_in(splits[3], 1), TOKENS // TOK_DEV)
    expert_ids_turns = jax.random.permutation(jax.random.fold_in(splits[3], 3), TOKENS // TOK_DEV)
    expert_ids = jax.vmap(lambda own, number: assign_block(jax.random.fold_in(splits[3], 2), own, number, TOK_DEV, EXPERTS, TOP, CAP, 0))(expert_ids_keys, expert_ids_turns).reshape((TOKENS, TOP))
    saved_gate = centred(splits[4], (FF, EXPERTS, SLOTS), 1.0, 6.0, ((1, 8),))
    saved_up = centred(splits[5], (FF, EXPERTS, SLOTS), 1.0, 6.0, ((1, 8),))
    w_gate = centred(splits[6], (EXPERTS, D, FF), FF ** -0.5, 0.1875, ((0, 8), (1, 4)))
    w_up = centred(splits[7], (EXPERTS, D, FF), FF ** -0.5, 0.1875, ((0, 8), (1, 4)))
    w_down = heavy_noise(splits[8], (EXPERTS, FF, D), FF ** -0.5, 0.25, ((0, 8), (2, 4)), (2, 1, 4, 2.0))
    return {"tokens": tokens, "cotangent": cotangent, "gates": gates, "expert_ids": expert_ids, "saved_gate": saved_gate, "saved_up": saved_up, "w_gate": w_gate, "w_up": w_up, "w_down": w_down}


def slot_codes(expert_ids, capacity, expert_count):
    tok_rows, top_count = expert_ids.shape
    flat = expert_ids.reshape(-1)
    onehot = (flat[:, None] == jnp.arange(expert_count, dtype=jnp.int32)[None, :]).astype(jnp.int32)
    before = jnp.cumsum(onehot, axis=0) - onehot
    position = jnp.sum(before * onehot, axis=1)
    return (flat * capacity + position).reshape(tok_rows, top_count)


def reference(tokens, cotangent, gates, expert_ids, saved_gate, saved_up, w_gate, w_up, w_down):
    source_count = N_EX * N_EY
    slot_total = source_count * CAP
    block_width = D // N_TP
    blocks = expert_ids.reshape(source_count, TOK_DEV, TOP)
    codes = jax.vmap(lambda stretch_ids: slot_codes(stretch_ids, CAP, EXPERTS))(blocks)
    position = codes - blocks * CAP
    source = jnp.arange(source_count, dtype=jnp.int32)[:, None, None]
    row_id = (blocks * slot_total + source * CAP + position).reshape(TOKENS, TOP).astype(jnp.int32)
    pair_index = jnp.arange(TOKENS * TOP, dtype=jnp.int32)
    table = jnp.full((EXPERTS * slot_total,), TOKENS * TOP, jnp.int32).at[row_id.reshape(-1)].set(pair_index)
    table = table.reshape(EXPERTS, slot_total)
    x_pad = jnp.concatenate([tokens, jnp.zeros((1, D), tokens.dtype)], axis=0)
    dy_pad = jnp.concatenate([cotangent, jnp.zeros((1, D), cotangent.dtype)], axis=0)
    g_pad = jnp.concatenate([gates.reshape(-1), jnp.zeros((1,), gates.dtype)], axis=0)
    gate_major = jnp.moveaxis(saved_gate, 1, 0)
    up_major = jnp.moveaxis(saved_up, 1, 0)

    def one_expert(bundle):
        pairs, weight_gate, weight_up, weight_down, gate_pre, up_pre = bundle
        token_row = pairs // TOP
        x_rows = x_pad[token_row]
        dy_rows = dy_pad[token_row]
        g_rows = g_pad[pairs]
        scaled = (g_rows.astype(jnp.float32)[:, None] * dy_rows.astype(jnp.float32)).astype(jnp.bfloat16)
        act_gate = gate_pre.astype(jnp.float32)
        act_up = up_pre.astype(jnp.float32)
        sigm = jax.nn.sigmoid(act_gate)
        hidden = (act_gate * sigm * act_up).astype(jnp.bfloat16)
        out_rows = lax.dot_general(hidden, weight_down, (((0,), (0,)), ((), ())), preferred_element_type=jnp.float32)
        prod = (dy_rows.astype(jnp.float32) * out_rows).reshape(slot_total, N_TP, block_width)
        score_part = lax.optimization_barrier(jnp.sum(prod, axis=2).astype(jnp.bfloat16))
        score = jnp.sum(score_part.astype(jnp.float32), axis=1).astype(jnp.bfloat16)
        down_blocks = weight_down.astype(jnp.float32).reshape(FF, N_TP, block_width)
        scaled_blocks = scaled.astype(jnp.float32).reshape(slot_total, N_TP, block_width)
        dh_part = jnp.einsum("fjd,sjd->jfs", down_blocks, scaled_blocks, precision=lax.Precision.HIGHEST)
        dh_part = lax.optimization_barrier(dh_part.astype(jnp.bfloat16))
        dh_sum = jnp.sum(dh_part.astype(jnp.float32), axis=0).astype(jnp.bfloat16)
        dh_wide = dh_sum.astype(jnp.float32)
        d_gate_pre = (dh_wide * act_up * sigm * (1.0 + act_gate * (1.0 - sigm))).astype(jnp.bfloat16)
        d_up_pre = (dh_wide * act_gate * sigm).astype(jnp.bfloat16)
        dims = (((0,), (1,)), ((), ()))
        dx_rows = lax.dot_general(d_gate_pre, weight_gate, dims, preferred_element_type=jnp.float32)
        dx_rows = dx_rows + lax.dot_general(d_up_pre, weight_up, dims, preferred_element_type=jnp.float32)
        grad_gate_w = lax.dot_general(x_rows, d_gate_pre, dims, preferred_element_type=jnp.float32)
        grad_up_w = lax.dot_general(x_rows, d_up_pre, dims, preferred_element_type=jnp.float32)
        grad_down_w = jnp.dot(hidden, scaled, preferred_element_type=jnp.float32)
        return (dx_rows.astype(jnp.bfloat16), score, grad_gate_w.astype(jnp.bfloat16),
                grad_up_w.astype(jnp.bfloat16), grad_down_w.astype(jnp.bfloat16))

    dx_all, score_all, grad_w_gate, grad_w_up, grad_w_down = lax.map(
        one_expert, (table, w_gate, w_up, w_down, gate_major, up_major))
    dx_flat = dx_all.reshape(EXPERTS * slot_total, D)
    total = jnp.zeros((TOKENS, D), jnp.float32)
    for choice_index in range(TOP):
        total = total + dx_flat[row_id[:, choice_index]].astype(jnp.float32)
    grad_tokens = total.astype(jnp.bfloat16)
    grad_gates = score_all.reshape(-1)[row_id]
    return grad_tokens, grad_gates, grad_w_gate, grad_w_up, grad_w_down
```

```python
import jax
import jax.numpy as jnp
from jax import lax
from jax.sharding import PartitionSpec as P

LANES = 128
GROUP = ("ex", "ey")


def scatter_blocks(blocks, parts):
    if parts > 4:
        got = lax.all_to_all(blocks, "tp", split_axis=0, concat_axis=0, tiled=True)
        return [got[i] for i in range(parts)]
    me = lax.axis_index("tp")
    got = [lax.dynamic_index_in_dim(blocks, me, 0, keepdims=False)]
    for step in range(1, parts):
        piece = lax.dynamic_index_in_dim(blocks, (me + step) % parts, 0, keepdims=False)
        got.append(lax.ppermute(piece, "tp", [(i, (i + step) % parts) for i in range(parts)]))
    return got


def block_sum(terms):
    return sum(term.astype(jnp.float32) for term in terms).astype(jnp.bfloat16)


def gather_pieces(block, parts):
    if parts > 4:
        return [lax.all_gather(block, "tp", axis=0)]
    shifts = [[(i, (i + step) % parts) for i in range(parts)] for step in range(1, parts)]
    return [block] + [lax.ppermute(block, "tp", shift) for shift in shifts]


def in_order(pieces, parts):
    if parts > 4:
        return pieces[0]
    me = lax.axis_index("tp")
    whole = jnp.zeros((parts,) + pieces[0].shape, pieces[0].dtype)
    for step, piece in enumerate(pieces):
        whole = lax.dynamic_update_index_in_dim(whole, piece, (me - step) % parts, 0)
    return whole


def on_device(tokens, cotangent, gates, expert_ids, saved_gate, saved_up, w_gate, w_up, w_down):
    groups = lax.axis_size(GROUP)
    parts = lax.axis_size("tp")
    rows, width = tokens.shape
    top = expert_ids.shape[1]
    hidden_units, local, slots = saved_gate.shape
    capacity = slots // groups
    total = groups * rows
    first = lax.axis_index(GROUP) * local

    extra = jnp.concatenate(
        [gates, expert_ids.astype(jnp.bfloat16), jnp.zeros((rows, LANES - 2 * top), jnp.bfloat16)],
        axis=1,
    )
    packed = jnp.concatenate([cotangent, extra], axis=1)
    packed = lax.all_gather(packed, GROUP, axis=0, tiled=True)
    tokens, packed = lax.optimization_barrier((tokens, packed))
    all_x = lax.all_to_all(
        jnp.broadcast_to(tokens[None], (groups, rows, width)),
        GROUP, split_axis=0, concat_axis=0, tiled=True,
    ).reshape(total, width)
    all_dy = packed[:, :width]
    small = packed[:, width:].astype(jnp.float32).T
    all_gates = small[:top]
    all_ids = small[top : 2 * top].astype(jnp.int32)

    match = all_ids[None] == first + jnp.arange(local, dtype=jnp.int32)[:, None, None]
    named = jnp.sum(match.astype(jnp.float32), axis=1)
    gate_of = jnp.sum(jnp.where(match, all_gates[None], 0.0), axis=1)
    place = jnp.arange(total, dtype=jnp.int32)
    group_of = place // rows
    earlier = (place[:, None] < place[None, :]) & (group_of[:, None] == group_of[None, :])
    position = jnp.dot(
        named.astype(jnp.bfloat16), earlier.astype(jnp.bfloat16), preferred_element_type=jnp.float32
    ).astype(jnp.int32)
    row_of = jnp.where(named > 0, group_of[None] * capacity + position, -1)
    taken = row_of[:, None, :] == jnp.arange(slots, dtype=jnp.int32)[None, :, None]
    chosen = taken.astype(jnp.bfloat16).reshape(local * slots, total)
    gate_rows = jnp.sum(jnp.where(taken, gate_of[:, None, :], 0.0), axis=2, keepdims=True)

    dy_rows = jnp.dot(chosen, all_dy, preferred_element_type=jnp.float32).astype(jnp.bfloat16)
    dy_rows = dy_rows.reshape(local, slots, width)
    halves = 2 if local % 2 == 0 else 1
    each = local // halves
    cuts = [slice(h * each, (h + 1) * each) for h in range(halves)]
    received = []
    for cut in cuts:
        raw = jnp.einsum(
            "erd,efd->erf", dy_rows[cut], w_down[cut], preferred_element_type=jnp.float32
        ).astype(jnp.bfloat16)
        raw = raw.reshape(parts, each * slots // parts, hidden_units)
        received.append(scatter_blocks(raw, parts))

    scaled = (gate_rows * dy_rows.astype(jnp.float32)).astype(jnp.bfloat16)
    act_gate = saved_gate.transpose(1, 2, 0).astype(jnp.float32)
    act_up = saved_up.transpose(1, 2, 0).astype(jnp.float32)
    sigm = jax.nn.sigmoid(act_gate)
    hidden = (act_gate * sigm * act_up).astype(jnp.bfloat16)
    sums = [block_sum(received[0])]
    hidden, scaled, sums[0] = lax.optimization_barrier((hidden, scaled, sums[0]))
    grad_w_down = jnp.einsum(
        "erf,erd->efd", hidden, scaled, preferred_element_type=jnp.float32
    ).astype(jnp.bfloat16)

    for terms in received[1:]:
        terms, grad_w_down = lax.optimization_barrier((terms, grad_w_down))
        sums.append(block_sum(terms))
    gathered = [gather_pieces(block, parts) for block in sums]
    d_gate, d_up, score, dx_rows = [], [], [], []
    for cut, pieces in zip(cuts, gathered):
        if dx_rows:
            pieces, dx_rows[-1] = lax.optimization_barrier((pieces, dx_rows[-1]))
        raw = in_order(pieces, parts).reshape(each, slots, hidden_units).astype(jnp.float32)
        a, u, q = act_gate[cut], act_up[cut], sigm[cut]
        dh = gate_rows[cut] * raw
        part_score = jnp.sum(raw * hidden[cut].astype(jnp.float32), axis=2, keepdims=True)
        part_gate = (dh * u * q * (1.0 + a * (1.0 - q))).astype(jnp.bfloat16)
        part_up = (dh * a * q).astype(jnp.bfloat16)
        part_gate, part_up = lax.optimization_barrier((part_gate, part_up))
        dx = jnp.einsum("erf,edf->erd", part_gate, w_gate[cut], preferred_element_type=jnp.float32)
        dx = dx + jnp.einsum("erf,edf->erd", part_up, w_up[cut], preferred_element_type=jnp.float32)
        dx_rows.append(dx.astype(jnp.bfloat16))
        d_gate.append(part_gate)
        d_up.append(part_up)
        score.append(part_score)
    d_gate, d_up, score, dx_rows = [
        jnp.concatenate(pieces, axis=0) for pieces in (d_gate, d_up, score, dx_rows)
    ]
    dx_rows = dx_rows.reshape(local * slots, width)
    own = jnp.arange(LANES)[None, None, :] == jnp.arange(local)[:, None, None]
    score_cols = jnp.where(own, score, 0.0).astype(jnp.bfloat16).reshape(local * slots, LANES)
    over_rows = (((0,), (0,)), ((), ()))
    back = [
        lax.dot_general(chosen, part, over_rows, preferred_element_type=jnp.float32).astype(
            jnp.bfloat16
        )
        for part in (dx_rows, score_cols)
    ]
    back = jnp.concatenate(back, axis=1).reshape(groups, rows, width + LANES)
    back = lax.all_to_all(back, GROUP, split_axis=0, concat_axis=0, tiled=True)

    x_rows = jnp.dot(chosen, all_x, preferred_element_type=jnp.float32).astype(jnp.bfloat16)
    x_rows = x_rows.reshape(local, slots, width)
    grad_w_gate = jnp.einsum(
        "erd,erf->edf", x_rows, d_gate, preferred_element_type=jnp.float32
    ).astype(jnp.bfloat16)
    grad_w_up = jnp.einsum(
        "erd,erf->edf", x_rows, d_up, preferred_element_type=jnp.float32
    ).astype(jnp.bfloat16)

    grad_tokens = jnp.sum(back[:, :, :width].astype(jnp.float32), axis=0).astype(jnp.bfloat16)
    table = back[:, :, width : width + local].transpose(1, 0, 2).reshape(rows, groups * local)
    picks = expert_ids[:, :, None] == jnp.arange(groups * local, dtype=jnp.int32)[None, None, :]
    grad_gates = jnp.sum(
        jnp.where(picks, table.astype(jnp.float32)[:, None, :], 0.0), axis=2
    ).astype(jnp.bfloat16)
    return (grad_tokens, grad_gates, grad_w_gate, grad_w_up, grad_w_down)


def solution(mesh):
    by_group = P(GROUP, "tp")
    small = P(GROUP, None)
    saved = P(None, GROUP, None)
    wide = P(GROUP, "tp", None)
    down = P(GROUP, None, "tp")
    in_specs = (by_group, by_group, small, small, saved, saved, wide, wide, down)
    out_specs = (by_group, small, wide, wide, down)
    return jax.shard_map(
        on_device, mesh=mesh, in_specs=in_specs, out_specs=out_specs, check_vma=False
    )
```
